1024 devices in a mesh: pair: 128 (over z_lo, y, core), aux: 8 (over x, z_hi).
Axes of the slice: x: 4, y: 8, z: 16 (z_hi: 2, z_lo: 8; z = z_hi * 8 + z_lo), core: 2. Of those that a mesh axis runs over, the one named last changes fastest.
Arguments:
- occupied_index: int32 [128], P('pair'), may hold values from 0 to 3
- doubles_slab: bfloat16 [128, 2048, 2048], P('pair', 'aux'), may hold values from -0.015625 to 0.015625
- lambda_slab: bfloat16 [128, 2048, 2048], P('pair', 'aux'), may hold values from -0.015625 to 0.015625
- aux_factors: bfloat16 [128, 256, 2048], P('pair'), may hold values from -24 to 24
- dressed_factors: bfloat16 [128, 256, 2048], P('pair'), may hold values from -6 to 6
- virtual_coefs: bfloat16 [1024, 2048], P(None, 'aux'), may hold values from -0.125 to 0.125
- occupied_coefs: float32 [512, 4], replicated, may hold values from -3 to 3
Outputs:
- gamma_basis: bfloat16 [256, 512, 1024], P('pair', None, 'aux')
The draws below stay inside these ranges and needn't reach their ends.
Inputs may be any that keep to these rules, and one draw needn't show every extreme that they name: `occupied_index`: entry p is the occupied index i that forms a pair with the occupied index j = p.
All inputs are finite; a program needn't handle non-finite values.
Results may differ from the reference program's by a relative error of at most 0.014.
Values may be sent and summed in bfloat16 or wider, within the bound.
A program may use at most 32 MiB of HBM per device.

```python
import jax
import jax.numpy as jnp
from jax import lax

V = 2048
I_WIN = 4
MU_WIN = 512
NU_WIN = 1024
Q_SLAB = 256
N_J = 128
N_PAIR = 128


def plant(drawn, key, least, high):
    dims = drawn.shape
    place = [jax.random.randint(jax.random.fold_in(key, axis), (), 0, dims[axis]) for axis in range(len(dims))]
    drawn = drawn.at[tuple(place)].set(least)
    longest = dims.index(max(dims))
    place[longest] = (place[longest] + 1) % dims[longest]
    return drawn.at[tuple(place)].set(high)


def with_spikes(result, stream_key, source, target, shards_of, factor):
    def block_of(axis_at):
        return (jnp.arange(result.shape[axis_at]) // (result.shape[axis_at] // shards_of)).reshape((-1,) + (1,) * (result.ndim - 1 - axis_at))

    one_side = jax.random.permutation(stream_key, shards_of)[block_of(target)]
    far = (block_of(target) + shards_of // 2) % shards_of
    return jnp.where((block_of(source) == one_side) | (block_of(source) == far), factor * result, result)


def shard_levels(own_key, dims, split, smallest, high):
    loudness, own = 1.0, jax.random.fold_in(own_key, 6)
    for position, parts in split:
        heights = jnp.exp(jax.random.uniform(jax.random.fold_in(own, position), (parts,), jnp.float32, smallest / len(split), high / len(split)))
        loudness = loudness * jnp.repeat(heights, dims[position] // parts).reshape([-1 if axis == position else 1 for axis in range(len(dims))])
    return loudness


def bell_draw(stream_key, extent, width, bound, shards=(), kind=jnp.bfloat16):
    result = width * jax.random.normal(stream_key, extent, jnp.float32)
    if shards:
        result = result * shard_levels(stream_key, extent, shards, -0.22, 0.18)
    return jnp.clip(result, -bound, bound).astype(kind)


def bell_draw_with(key, dims, deviation, reach, split, heavy, held_as=jnp.bfloat16):
    drawn = deviation * jax.random.normal(key, dims, jnp.float32)
    if split:
        drawn = drawn * shard_levels(key, dims, split, -0.22, 0.18)
    return jnp.clip(with_spikes(drawn, jax.random.fold_in(key, 3), *heavy), -reach, reach).astype(held_as)


def setup_inputs(seed: int = 0) -> dict:
    key_of = jax.random.split(jax.random.key(seed), 8)
    return {
        "occupied_index": plant(jax.random.randint(key_of[0], (N_J,), 0, I_WIN), jax.random.fold_in(key_of[0], 1), 0, I_WIN - 1).astype(jnp.int32),
        "doubles_slab": bell_draw(key_of[1], (N_J, V, V), (2 * V * N_PAIR // I_WIN) ** -0.5, 0.015625, ((0, 128), (1, 8))),
        "lambda_slab": bell_draw(key_of[2], (N_J, V, V), (2 * V * N_PAIR // I_WIN) ** -0.5, 0.015625, ((0, 128), (1, 8))),
        "aux_factors": bell_draw_with(key_of[3], (N_J, Q_SLAB, V), 1.0, 24.0, ((0, 128),), (0, 1, 128, 5.5)),
        "dressed_factors": bell_draw(key_of[4], (N_J, Q_SLAB, V), 1.0, 6.0, ((0, 128),)),
        "virtual_coefs": bell_draw(key_of[5], (NU_WIN, V), V ** -0.5, 0.125, ((1, 8),)),
        "occupied_coefs": bell_draw(key_of[6], (MU_WIN, I_WIN), I_WIN ** -0.5, 3.0, (), jnp.float32),
    }


def reference(occupied_index, doubles_slab, lambda_slab, aux_factors, dressed_factors, virtual_coefs, occupied_coefs):
    highest = lax.Precision.HIGHEST

    def add_pair(total, items):
        index, doubles, lambdas, factors, dressed = items
        product = jnp.dot(factors.astype(jnp.float32), doubles.astype(jnp.float32).T, precision=highest)
        product = product + jnp.dot(dressed.astype(jnp.float32), lambdas.astype(jnp.float32).T, precision=highest)
        return total.at[:, index, :].add(product), None

    initial = jnp.zeros((Q_SLAB, I_WIN, V), jnp.float32)
    summed, _ = lax.scan(add_pair, initial, (occupied_index.astype(jnp.int32), doubles_slab, lambda_slab, aux_factors, dressed_factors))
    gamma_mo = summed.astype(jnp.bfloat16)
    virtual_half = jnp.einsum("qia,na->qin", gamma_mo.astype(jnp.float32), virtual_coefs.astype(jnp.float32), precision=highest)

    def one_slab(half_rows):
        return jnp.dot(occupied_coefs, half_rows, precision=highest).astype(jnp.bfloat16)

    return lax.map(one_slab, virtual_half)
```

```python
import functools

import jax
import jax.numpy as jnp
from jax import lax
from jax.experimental import pallas as pl
from jax.experimental.pallas import tpu as pltpu
from jax.sharding import PartitionSpec as P

MESH = pl.DeviceIdType.MESH
F32, BF16 = jnp.float32, jnp.bfloat16
NT = (((1,), (1,)), ((), ()))
NX, NY, NZ, ZL = 4, 8, 16, 8
NR = 2 * NY


def device(x, y, z, core):
    pair = (lax.rem(z, ZL) * NY + y) * 2 + core
    aux = x * 2 + lax.div(z, ZL)
    return (pair, aux)


def kernel(
    idx_hbm, d_hbm, l_hbm, f_hbm, g_hbm, v_hbm, c_hbm, out_ref,
    idx_s, d_v, l_v, f_v, g_v, v_v, c_v,
    prod, idx_send, idx_recv, y_send, y_recv, sel, own_t, x_send, x_recv,
    total, z_send, z_recv, wide, left,
    load_sem, idx_sem, y_sem, x_sem, z_sem, ready_sem,
):
    pair, aux = lax.axis_index("pair"), lax.axis_index("aux")
    core = lax.rem(pair, 2)
    y = lax.rem(lax.div(pair, 2), NY)
    x = lax.div(aux, 2)
    z = lax.rem(aux, 2) * ZL + lax.div(pair, NR)
    barrier = pltpu.get_barrier_semaphore()

    def rel_y(dy, dc):
        return lax.rem(y + dy, NY), lax.rem(core + dc, 2)

    def dev_y(dy, dc):
        to_y, to_core = rel_y(dy, dc)
        return device(x, to_y, z, to_core)

    def dev_x(dx):
        return device(lax.rem(x + dx, NX), y, z, core)

    def dev_z(dz):
        return device(x, y, lax.rem(z + dz, NZ), core)

    def greet(to):
        pl.semaphore_signal(barrier, inc=1, device_id=to, device_id_type=MESH)

    @pl.loop(1, NR)
    def _(s):
        greet(dev_y(lax.div(s, 2), lax.rem(s, 2)))

    @pl.loop(1, NX)
    def _(s):
        greet(dev_x(s))

    @pl.loop(1, 5)
    def _(s):
        greet(dev_z(s))
        greet(dev_z(NZ - s))

    def load(src, dst, n):
        return pltpu.make_async_copy(src, dst, load_sem.at[n])

    half = d_v.shape[1] // 2
    loads = []
    for n, (a_hbm, a_v) in enumerate(((d_hbm, d_v), (f_hbm, f_v), (l_hbm, l_v), (g_hbm, g_v))):
        for k in range(2):
            cols = pl.ds(k * half, half)
            loads.append(load(a_hbm.at[0, :, cols], a_v.at[:, cols], n * 2 + k))
    for n in (0, 2, 1, 3, 4, 6, 5, 7):
        loads[n].start()
    load_v = load(v_hbm, v_v, 8)
    load_c = load(c_hbm, c_v, 9)
    load_i = load(idx_hbm, idx_s, 10)
    load_i.start()
    load_v.start()
    load_c.start()

    load_i.wait()
    idx_send[...] = jnp.full((1, 128), idx_s[0], jnp.int32)
    idx_recv[0] = jnp.full((1, 128), idx_s[0], jnp.int32)

    acc = None
    for n, (a_v, b_v) in enumerate(((f_v, d_v), (g_v, l_v))):
        for k in range(2):
            loads[n * 4 + k].wait()
            loads[n * 4 + 2 + k].wait()
            cols = slice(k * half, (k + 1) * half)
            part = lax.dot_general(a_v[:, cols], b_v[:, cols], NT, preferred_element_type=F32)
            acc = part if acc is None else acc + part
    prod[0] = acc[:, :128]
    prod[1] = acc[:, 128:]

    for r in range(NR):
        for j in range(2):
            even = prod[j, pl.ds(2 * r, 8, stride=32), :]
            odd = prod[j, pl.ds(2 * r + 1, 8, stride=32), :]
            both = jnp.concatenate([even, odd], axis=0).astype(BF16)
            y_send[r, :, j * 128 : (j + 1) * 128] = both
    y_recv[0] = y_send[y * 2 + core]

    pl.semaphore_wait(barrier, NR - 1 + NX - 1 + 8)

    for dz in (4, NZ - 4):
        pl.semaphore_signal(ready_sem, inc=1, device_id=dev_z(dz), device_id_type=MESH)

    def send_idx(dy, dc):
        pltpu.make_async_remote_copy(
            src_ref=idx_send, dst_ref=idx_recv.at[dy * 2 + dc],
            send_sem=idx_sem.at[0], recv_sem=idx_sem.at[1],
            device_id=dev_y(dy, dc), device_id_type=MESH,
        ).start()

    def send_y(dy, dc):
        to_y, to_core = rel_y(dy, dc)
        pltpu.make_async_remote_copy(
            src_ref=y_send.at[to_y * 2 + to_core], dst_ref=y_recv.at[dy * 2 + dc],
            send_sem=y_sem.at[0], recv_sem=y_sem.at[1],
            device_id=dev_y(dy, dc), device_id_type=MESH,
        ).start()

    def far_first(k):
        step = lax.div(k + 1, 2)
        return 4 + step - 2 * step * lax.rem(k, 2)

    for send in (send_idx, send_y):
        @pl.loop(0, NY - 1)
        def _(k):
            send(far_first(k), 0)
            send(far_first(k), 1)

        send(0, 1)

    load_c.wait()
    wide[...] = jnp.zeros_like(wide)
    c_hi = c_v[...].astype(BF16).astype(F32)
    c_lo = (c_v[...] - c_hi)
    for e in range(2):
        cols = slice(e * 512, (e + 1) * 512)
        for i in range(4):
            row = i * 2 + e
            wide[row : row + 1, cols] = c_hi[i : i + 1, :]
            wide[8 + row : 9 + row, cols] = c_hi[i : i + 1, :]
            wide[16 + row : 17 + row, cols] = c_lo[i : i + 1, :]
    left[...] = wide[...].T.astype(BF16)

    pltpu.make_async_copy(idx_recv.at[pl.ds(1, NR - 1)], idx_recv.at[pl.ds(1, NR - 1)], idx_sem.at[1]).wait()
    row = lax.broadcasted_iota(jnp.int32, (64, 256), 0)
    col = lax.broadcasted_iota(jnp.int32, (64, 256), 1)
    same = ((row >> 3) == (col & 7)) & ((row & 1) == ((col >> 3) & 1))
    lane = lax.broadcasted_iota(jnp.int32, (1, 128), 1) >> 4
    held = []
    for j in range(2):
        which = jnp.zeros((1, 128), jnp.int32)
        for s in range(8):
            which = which + idx_recv[j * 8 + s] * (lane == s).astype(jnp.int32)
        held.append(which)
    which = jnp.concatenate(held, axis=1)
    match = same.astype(F32) * (which == ((row >> 1) & 3)).astype(F32)
    sel[...] = match.astype(BF16)
    load_v.wait()

    pltpu.make_async_copy(y_recv.at[pl.ds(1, NR - 1)], y_recv.at[pl.ds(1, NR - 1)], y_sem.at[1]).wait()
    arrived = y_recv[...].reshape(256, 256)
    summed = jnp.dot(sel[...], arrived, preferred_element_type=F32).astype(BF16)

    def copy_x(dx):
        return pltpu.make_async_remote_copy(
            src_ref=x_send.at[dx - 1], dst_ref=x_recv.at[dx - 1],
            send_sem=x_sem.at[0, dx - 1], recv_sem=x_sem.at[1, dx - 1],
            device_id=dev_x(dx), device_id_type=MESH,
        )

    def turned(dx):
        rows = pl.ds(pl.multiple_of(lax.rem(x + dx, NX) * 256, 256), 256)
        return lax.dot_general(summed, v_v[rows, :], NT, preferred_element_type=F32)

    for dx in (2, 1, 3):
        x_send[dx - 1] = turned(dx).astype(BF16)
    for dx in (2, 1, 3):
        copy_x(dx).start()
    mine = turned(0)
    for dx in (1, 3, 2):
        copy_x(dx).wait_recv()
        mine = mine + x_recv[dx - 1].astype(F32)
    total[...] = mine.reshape(8, 8, 256)

    def z_block(dz):
        to_z = lax.rem(z + dz, NZ)
        cols = pl.ds(pl.multiple_of(lax.div(to_z, ZL) * 128, 128), 128)
        return total[lax.rem(to_z, ZL), :, cols]

    for dz in range(1, NZ):
        z_send[dz] = z_block(dz).astype(BF16)
    pl.semaphore_wait(ready_sem, 2)

    @pl.loop(0, NZ - 1)
    def _(k):
        step = lax.div(k + 1, 2)
        dz = 8 + step - 2 * step * lax.rem(k, 2)
        pltpu.make_async_remote_copy(
            src_ref=z_send.at[dz], dst_ref=z_recv.at[dz],
            send_sem=z_sem.at[0], recv_sem=z_sem.at[1],
            device_id=dev_z(dz), device_id_type=MESH,
        ).start()

    got = z_block(0)
    pltpu.make_async_copy(y_recv.at[pl.ds(1, NR - 1)], y_recv.at[pl.ds(1, NR - 1)], y_sem.at[0]).wait()
    pltpu.make_async_copy(idx_recv.at[pl.ds(1, NR - 1)], idx_recv.at[pl.ds(1, NR - 1)], idx_sem.at[0]).wait()
    for dx in (1, 2, 3):
        copy_x(dx).wait_send()

    z_in = z_recv.at[pl.ds(1, NZ - 1)]
    pltpu.make_async_copy(z_in, z_in, z_sem.at[1]).wait()
    for dz in range(1, NZ):
        got = got + z_recv[dz].astype(F32)
    hi = got.astype(BF16).astype(F32)
    right = jnp.concatenate([hi, got - hi, hi, jnp.zeros((104, 128), F32)], axis=0).astype(BF16)
    result = jnp.dot(left[...], right, preferred_element_type=F32)
    out_ref[...] = result.astype(BF16).reshape(2, 512, 128)
    pltpu.make_async_copy(z_in, z_in, z_sem.at[0]).wait()


def shards(
    occupied_index,
    doubles_slab,
    lambda_slab,
    aux_factors,
    dressed_factors,
    virtual_coefs,
    occupied_coefs,
):
    dma = pltpu.SemaphoreType.DMA
    return pl.pallas_call(
        kernel,
        out_shape=jax.ShapeDtypeStruct((2, 512, 128), BF16),
        in_specs=[pl.BlockSpec(memory_space=pltpu.HBM)] * 7,
        out_specs=pl.BlockSpec(memory_space=pltpu.VMEM),
        scratch_shapes=[
            pltpu.SMEM((1,), jnp.int32),
            pltpu.VMEM((256, 2048), BF16),
            pltpu.VMEM((256, 2048), BF16),
            pltpu.VMEM((256, 2048), BF16),
            pltpu.VMEM((256, 2048), BF16),
            pltpu.VMEM((1024, 256), BF16),
            pltpu.VMEM((4, 512), F32),
            pltpu.VMEM((2, 256, 128), F32),
            pltpu.VMEM((1, 128), jnp.int32),
            pltpu.VMEM((NR, 1, 128), jnp.int32),
            pltpu.VMEM((NR, 16, 256), BF16),
            pltpu.VMEM((NR, 16, 256), BF16),
            pltpu.VMEM((64, 256), BF16),
            pltpu.VMEM((8, 128), F32),
            pltpu.VMEM((NX - 1, 64, 256), BF16),
            pltpu.VMEM((NX - 1, 64, 256), BF16),
            pltpu.VMEM((8, 8, 256), F32),
            pltpu.VMEM((NZ, 8, 128), BF16),
            pltpu.VMEM((NZ, 8, 128), BF16),
            pltpu.VMEM((128, 1024), F32),
            pltpu.VMEM((1024, 128), BF16),
            dma((11,)),
            dma((2,)),
            dma((2,)),
            dma((2, NX - 1)),
            dma((2,)),
            pltpu.SemaphoreType.REGULAR,
        ],
        compiler_params=pltpu.CompilerParams(
            collective_id=0, has_side_effects=True, vmem_limit_bytes=32 << 20
        ),
    )(
        occupied_index, doubles_slab, lambda_slab, aux_factors, dressed_factors,
        virtual_coefs, occupied_coefs.T,
    )


def solution(mesh):
    placed = (
        P("pair"),
        P("pair", "aux", None),
        P("pair", "aux", None),
        P("pair", None, None),
        P("pair", None, None),
        P(None, "aux"),
        P(),
    )
    return jax.shard_map(
        shards, mesh=mesh, in_specs=placed, out_specs=P("pair", None, "aux"), check_vma=False
    )
```

```python
import jax
import jax.numpy as jnp
from jax import lax
from jax.experimental import pallas as pl
from jax.experimental.pallas import tpu as pltpu
from jax.sharding import PartitionSpec as P

MESH = pl.DeviceIdType.MESH
F32, BF16 = jnp.float32, jnp.bfloat16
NT = (((1,), (1,)), ((), ()))
NX, NY, NZ, ZL = 4, 8, 16, 8
NR = 2 * NY
VMEM_KIB = 60 << 10


def device(x, y, z, core):
    pair = (lax.rem(z, ZL) * NY + y) * 2 + core
    aux = x * 2 + lax.div(z, ZL)
    return (pair, aux)


def kernel(
    idx_hbm, d_hbm, l_hbm, f_hbm, g_hbm, v_hbm, c_hbm, out_ref,
    idx_s, d_v, l_v, f_v, g_v, v_v, c_v,
    prod, idx_send, idx_recv, y_send, y_recv, sel, x_send, x_recv,
    total, z_send, z_recv, wide, left,
    load_sem, idx_sem, y_sem, x_sem, z_sem, ready_sem,
):
    pair, aux = lax.axis_index("pair"), lax.axis_index("aux")
    core = lax.rem(pair, 2)
    y = lax.rem(lax.div(pair, 2), NY)
    x = lax.div(aux, 2)
    z = lax.rem(aux, 2) * ZL + lax.div(pair, NR)
    barrier = pltpu.get_barrier_semaphore()

    def rel_y(dy, dc):
        return lax.rem(y + dy, NY), lax.rem(core + dc, 2)

    def dev_y(dy, dc):
        to_y, to_core = rel_y(dy, dc)
        return device(x, to_y, z, to_core)

    def dev_x(dx):
        return device(lax.rem(x + dx, NX), y, z, core)

    def dev_z(dz):
        return device(x, y, lax.rem(z + dz, NZ), core)

    def greet(to):
        pl.semaphore_signal(barrier, inc=1, device_id=to, device_id_type=MESH)

    @pl.loop(1, NR)
    def _(s):
        greet(dev_y(lax.div(s, 2), lax.rem(s, 2)))

    @pl.loop(1, NX)
    def _(s):
        greet(dev_x(s))

    @pl.loop(1, 5)
    def _(s):
        greet(dev_z(s))
        greet(dev_z(NZ - s))

    def load(src, dst, n):
        return pltpu.make_async_copy(src, dst, load_sem.at[n])

    load_i = load(idx_hbm, idx_s, 0)
    load_i.start()
    depth = d_v.shape[1] // 2
    loads = []
    for a_hbm, a_v, b_hbm, b_v in ((f_hbm, f_v, d_hbm, d_v), (g_hbm, g_v, l_hbm, l_v)):
        for k in range(2):
            cols = pl.ds(k * depth, depth)
            top = pl.ds(0, 128)
            n = 1 + 2 * len(loads)
            loads.append((
                load(b_hbm.at[0, :, cols], b_v.at[:, cols], n),
                load(a_hbm.at[0, top, cols], a_v.at[top, cols], n + 1),
            ))
    rest = pl.ds(128, 128)
    later = [
        load(f_hbm.at[0, rest, :], f_v.at[rest, :], 9),
        load(g_hbm.at[0, rest, :], g_v.at[rest, :], 10),
    ]
    load_v = load(v_hbm, v_v, 11)
    load_c = load(c_hbm, c_v, 12)
    for pair_of in loads:
        for one in pair_of:
            one.start()
    for one in later:
        one.start()
    load_v.start()
    load_c.start()

    def pack(t, acc):
        prod[0] = acc[:, :128]
        prod[1] = acc[:, 128:]
        for r in range(NR):
            for j in range(2):
                even = prod[j, pl.ds(2 * r, 4, stride=32), :]
                odd = prod[j, pl.ds(2 * r + 1, 4, stride=32), :]
                both = jnp.concatenate([even, odd], axis=0).astype(BF16)
                y_send[t, r, :, j * 128 : (j + 1) * 128] = both
        y_recv[t, 0] = y_send[t, y * 2 + core]

    def send_y(t, to_y, to_core):
        dy, dc = lax.rem(to_y - y + NY, NY), lax.rem(to_core + core, 2)
        slot = dy * 2 + dc

        @pl.when(slot != 0)
        def _():
            to = device(x, to_y, z, to_core)
            if t == 0:
                pltpu.make_async_remote_copy(
                    src_ref=idx_send, dst_ref=idx_recv.at[slot],
                    send_sem=idx_sem.at[0], recv_sem=idx_sem.at[1],
                    device_id=to, device_id_type=MESH,
                ).start()
            pltpu.make_async_remote_copy(
                src_ref=y_send.at[t, to_y * 2 + to_core], dst_ref=y_recv.at[t, slot],
                send_sem=y_sem.at[0, t], recv_sem=y_sem.at[1, t],
                device_id=to, device_id_type=MESH,
            ).start()

    def send_all_y(t):
        @pl.loop(0, NY // 2)
        def _(k):
            send_y(t, k, 0)
            send_y(t, k, 1)

        @pl.loop(0, NY // 2)
        def _(k):
            send_y(t, NY - 1 - k, 0)
            send_y(t, NY - 1 - k, 1)

    acc = None
    for n, (load_b, load_a) in enumerate(loads):
        load_b.wait()
        load_a.wait()
        a_v, b_v = ((f_v, d_v), (g_v, l_v))[n // 2]
        cols = slice(n % 2 * depth, (n % 2 + 1) * depth)
        part = lax.dot_general(a_v[:128, cols], b_v[:, cols], NT, preferred_element_type=F32)
        acc = part if acc is None else acc + part
    pack(0, acc)
    load_i.wait()
    idx_send[...] = jnp.full((1, 128), idx_s[0, 0], jnp.int32)
    idx_recv[0] = jnp.full((1, 128), idx_s[0, 0], jnp.int32)

    pl.semaphore_wait(barrier, NR - 1 + NX - 1 + 8)
    send_all_y(0)
    for dz in (4, NZ - 4):
        pl.semaphore_signal(ready_sem, inc=1, device_id=dev_z(dz), device_id_type=MESH)

    later[0].wait()
    acc = lax.dot_general(f_v[128:, :], d_v[...], NT, preferred_element_type=F32)
    later[1].wait()
    acc = acc + lax.dot_general(g_v[128:, :], l_v[...], NT, preferred_element_type=F32)
    pack(1, acc)
    send_all_y(1)

    load_c.wait()
    wide[...] = jnp.zeros_like(wide)
    c_hi = c_v[...].astype(BF16).astype(F32)
    c_lo = (c_v[...] - c_hi)
    for e in range(2):
        cols = slice(e * 512, (e + 1) * 512)
        for i in range(4):
            row = i * 2 + e
            wide[row : row + 1, cols] = c_hi[i : i + 1, :]
            wide[8 + row : 9 + row, cols] = c_hi[i : i + 1, :]
            wide[16 + row : 17 + row, cols] = c_lo[i : i + 1, :]
    left[...] = wide[...].T.astype(BF16)

    others = idx_recv.at[pl.ds(1, NR - 1)]
    pltpu.make_async_copy(others, others, idx_sem.at[1]).wait()
    row = lax.broadcasted_iota(jnp.int32, (32, 128), 0)
    col = lax.broadcasted_iota(jnp.int32, (32, 128), 1)
    same = ((row >> 3) == (col & 3)) & ((row & 1) == ((col >> 2) & 1))
    lane = lax.broadcasted_iota(jnp.int32, (1, 128), 1) >> 3
    which = jnp.zeros((1, 128), jnp.int32)
    for s in range(NR):
        which = which + idx_recv[s] * (lane == s).astype(jnp.int32)
    match = same.astype(F32) * (which == ((row >> 1) & 3)).astype(F32)
    sel[...] = match.astype(BF16)
    load_v.wait()

    def copy_x(t, hi, dx):
        return pltpu.make_async_remote_copy(
            src_ref=x_send.at[t, hi, dx - 1], dst_ref=x_recv.at[t, hi, dx - 1],
            send_sem=x_sem.at[0, t, hi, dx - 1], recv_sem=x_sem.at[1, t, hi, dx - 1],
            device_id=dev_x(dx), device_id_type=MESH,
        )

    own = {}

    def turn(t):
        others = y_recv.at[t, pl.ds(1, NR - 1)]
        pltpu.make_async_copy(others, others, y_sem.at[1, t]).wait()
        arrived = y_recv[t].reshape(128, 256)
        summed = jnp.dot(sel[...], arrived, preferred_element_type=F32).astype(BF16)

        def turned(hi, dx):
            first = lax.rem(x + dx, NX) * 256 + hi * 128
            rows = pl.ds(pl.multiple_of(first, 128), 128)
            return lax.dot_general(summed, v_v[rows, :], NT, preferred_element_type=F32)

        for hi in range(2):
            for dx in (2, 1, 3):
                x_send[t, hi, dx - 1] = turned(hi, dx).astype(BF16)
            for dx in (2, 1, 3):
                copy_x(t, hi, dx).start()
        for hi in range(2):
            own[t, hi] = turned(hi, 0)

    def pass_on(t, hi):
        mine = own[t, hi]
        for dx in (1, 3, 2):
            copy_x(t, hi, dx).wait_recv()
            mine = mine + x_recv[t, hi, dx - 1].astype(F32)
        blocks = mine.reshape(4, 8, 128)
        total[hi, t * 4 : t * 4 + 4] = blocks
        z_send[hi, t * 4 : t * 4 + 4] = blocks.astype(BF16)

    def send_z(t, hi):
        @pl.loop(t * 4, t * 4 + 4)
        def _(to_l):
            to_z = hi * ZL + to_l
            dz = lax.rem(to_z - z + NZ, NZ)

            @pl.when(dz != 0)
            def _():
                pltpu.make_async_remote_copy(
                    src_ref=z_send.at[hi, to_l], dst_ref=z_recv.at[dz],
                    send_sem=z_sem.at[0], recv_sem=z_sem.at[1],
                    device_id=dev_z(dz), device_id_type=MESH,
                ).start()

    turn(0)
    pass_on(0, 0)
    pl.semaphore_wait(ready_sem, 2)
    send_z(0, 0)
    turn(1)
    for t, hi in ((0, 1), (1, 0), (1, 1)):
        pass_on(t, hi)
        send_z(t, hi)

    got = total[lax.div(z, ZL), lax.rem(z, ZL)]
    pltpu.make_async_copy(others, others, idx_sem.at[0]).wait()
    for t in range(2):
        sent = y_recv.at[t, pl.ds(1, NR - 1)]
        pltpu.make_async_copy(sent, sent, y_sem.at[0, t]).wait()
        for hi in range(2):
            for dx in (1, 2, 3):
                copy_x(t, hi, dx).wait_send()

    z_in = z_recv.at[pl.ds(1, NZ - 1)]
    pltpu.make_async_copy(z_in, z_in, z_sem.at[1]).wait()
    for dz in range(1, NZ):
        got = got + z_recv[dz].astype(F32)
    hi = got.astype(BF16).astype(F32)
    right = jnp.concatenate([hi, got - hi, hi, jnp.zeros((104, 128), F32)], axis=0).astype(BF16)
    result = jnp.dot(left[...], right, preferred_element_type=F32)
    out_ref[...] = result.astype(BF16).reshape(2, 512, 128)
    pltpu.make_async_copy(z_in, z_in, z_sem.at[0]).wait()


def shards(
    occupied_index,
    doubles_slab,
    lambda_slab,
    aux_factors,
    dressed_factors,
    virtual_coefs,
    occupied_coefs,
):
    dma = pltpu.SemaphoreType.DMA
    return pl.pallas_call(
        kernel,
        out_shape=pltpu.VMEM((2, 512, 128), BF16),
        in_specs=[pl.BlockSpec(memory_space=pltpu.HBM)] * 7,
        out_specs=pl.BlockSpec(memory_space=pltpu.VMEM),
        scratch_shapes=[
            pltpu.SMEM((1, 1), jnp.int32),
            pltpu.VMEM((256, 2048), BF16),
            pltpu.VMEM((256, 2048), BF16),
            pltpu.VMEM((256, 2048), BF16),
            pltpu.VMEM((256, 2048), BF16),
            pltpu.VMEM((1024, 256), BF16),
            pltpu.VMEM((4, 512), F32),
            pltpu.VMEM((2, 128, 128), F32),
            pltpu.VMEM((1, 128), jnp.int32),
            pltpu.VMEM((NR, 1, 128), jnp.int32),
            pltpu.VMEM((2, NR, 8, 256), BF16),
            pltpu.VMEM((2, NR, 8, 256), BF16),
            pltpu.VMEM((32, 128), BF16),
            pltpu.VMEM((2, 2, NX - 1, 32, 128), BF16),
            pltpu.VMEM((2, 2, NX - 1, 32, 128), BF16),
            pltpu.VMEM((2, 8, 8, 128), F32),
            pltpu.VMEM((2, 8, 8, 128), BF16),
            pltpu.VMEM((NZ, 8, 128), BF16),
            pltpu.VMEM((128, 1024), F32),
            pltpu.VMEM((1024, 128), BF16),
            dma((13,)),
            dma((2,)),
            dma((2, 2)),
            dma((2, 2, 2, NX - 1)),
            dma((2,)),
            pltpu.SemaphoreType.REGULAR,
        ],
        compiler_params=pltpu.CompilerParams(
            collective_id=0, has_side_effects=True, vmem_limit_bytes=VMEM_KIB << 10
        ),
    )(
        occupied_index.reshape(1, 1), doubles_slab, lambda_slab, aux_factors, dressed_factors,
        virtual_coefs, occupied_coefs.T,
    )


def solution(mesh):
    placed = (
        P("pair"),
        P("pair", "aux", None),
        P("pair", "aux", None),
        P("pair", None, None),
        P("pair", None, None),
        P(None, "aux"),
        P(),
    )
    return jax.shard_map(
        shards, mesh=mesh, in_specs=placed, out_specs=P("pair", None, "aux"), check_vma=False
    )
```

```python
import jax
import jax.numpy as jnp
from jax import lax
from jax.experimental import pallas as pl
from jax.experimental.pallas import tpu as pltpu
from jax.sharding import PartitionSpec as P

MESH = pl.DeviceIdType.MESH
F32, BF16 = jnp.float32, jnp.bfloat16
NT = (((1,), (1,)), ((), ()))
NX, NY, NZ, ZL = 4, 8, 16, 8
NR = 2 * NY
Y_ORDER = (0, 1, 2, 3, 7, 6, 5, 4)
X_ORDER = (0, 1, 2, 3)


def kernel(
    idx_hbm, d_hbm, l_hbm, f_hbm, g_hbm, v_hbm, c_hbm, out_ref,
    idx_s, d_v, l_v, f_v, g_v, v_v, c_v,
    order, idx_send, idx_recv, y_send, y_recv, sel, x_send, x_recv,
    z_send, z_recv, wide, left,
    load_sem, idx_sem, y_sem, x_sem, z_sem, ready_sem,
):
    pair, aux = lax.axis_index("pair"), lax.axis_index("aux")
    barrier = pltpu.get_barrier_semaphore()

    def load(src, dst, n):
        return pltpu.make_async_copy(src, dst, load_sem.at[n])

    depth = d_v.shape[1] // 2
    loads = []
    for a_hbm, a_v, b_hbm, b_v in ((f_hbm, f_v, d_hbm, d_v), (g_hbm, g_v, l_hbm, l_v)):
        for k in range(2):
            cols = pl.ds(k * depth, depth)
            top = pl.ds(0, 128)
            n = 1 + 2 * len(loads)
            loads.append((
                load(b_hbm.at[0, :, cols], b_v.at[:, cols], n),
                load(a_hbm.at[0, top, cols], a_v.at[top, cols], n + 1),
            ))
    rest = pl.ds(128, 128)
    later = [
        load(f_hbm.at[0, rest, :], f_v.at[rest, :], 9),
        load(g_hbm.at[0, rest, :], g_v.at[rest, :], 10),
    ]
    load_i = load(idx_hbm, idx_s, 0)
    load_v = [load(v_hbm.at[:, hi], v_v.at[hi], 11 + hi) for hi in range(2)]
    load_c = load(c_hbm, c_v, 13)
    for pair_of in loads:
        for one in pair_of:
            one.start()
    load_i.start()

    r = lax.rem(pair, NR)
    l = lax.div(pair, NR)
    x = lax.div(aux, 2)
    h = lax.rem(aux, 2)
    z = h * ZL + l
    row0 = l * NR

    def z_away(dz):
        to_z = lax.rem(z + (dz + NZ), NZ)
        to_h = lax.div(to_z, ZL)
        return ((to_z - to_h * ZL) * NR + r, x * 2 + to_h)

    def greet(to):
        pl.semaphore_signal(barrier, inc=1, device_id=to, device_id_type=MESH)

    for to_r in range(NR):
        @pl.when(r != to_r)
        def _():
            greet((row0 + to_r, aux))

    for to_x in range(NX):
        @pl.when(x != to_x)
        def _():
            greet((pair, to_x * 2 + h))

    for dz in range(1, 3):
        greet(z_away(dz))
        greet(z_away(-dz))

    for one in later + load_v + [load_c]:
        one.start()

    row = lax.broadcasted_iota(jnp.int32, (128, 128), 0)
    col = lax.broadcasted_iota(jnp.int32, (128, 128), 1)
    source = (row & 3) * 32 + (row >> 3) * 2 + ((row >> 2) & 1)
    order[...] = (source == col).astype(F32).astype(BF16)

    def pack(t, acc):
        sorted_rows = jnp.dot(order[...], acc.astype(BF16), preferred_element_type=F32)
        y_send[t] = sorted_rows.astype(BF16).reshape(NR, 8, 256)
        y_recv[t, r] = y_send[t, r]

    def send_y(t):
        for to_r in (2 * to_y + c for to_y in Y_ORDER for c in range(2)):
            @pl.when(r != to_r)
            def _():
                to = (row0 + to_r, aux)
                if t == 0:
                    pltpu.make_async_remote_copy(
                        src_ref=idx_send, dst_ref=idx_recv.at[r],
                        send_sem=idx_sem.at[0], recv_sem=idx_sem.at[1],
                        device_id=to, device_id_type=MESH,
                    ).start()
                pltpu.make_async_remote_copy(
                    src_ref=y_send.at[t, to_r], dst_ref=y_recv.at[t, r],
                    send_sem=y_sem.at[0, t], recv_sem=y_sem.at[1, t],
                    device_id=to, device_id_type=MESH,
                ).start()

    def relay(n, dz):
        for to in (z_away(dz), z_away(-dz)):
            pl.semaphore_signal(ready_sem.at[n], inc=1, device_id=to, device_id_type=MESH)

    def settle(ref, sem):
        pltpu.make_async_copy(ref, ref, sem).wait()

    acc = None
    for n, (load_b, load_a) in enumerate(loads):
        load_b.wait()
        load_a.wait()
        a_v, b_v = ((f_v, d_v), (g_v, l_v))[n // 2]
        cols = slice(n % 2 * depth, (n % 2 + 1) * depth)
        part = lax.dot_general(a_v[:128, cols], b_v[:, cols], NT, preferred_element_type=F32)
        acc = part if acc is None else acc + part
    pack(0, acc)
    load_i.wait()
    idx_send[...] = jnp.full((1, 128), idx_s[0, 0], jnp.int32)
    idx_recv[r] = jnp.full((1, 128), idx_s[0, 0], jnp.int32)

    pl.semaphore_wait(barrier, NR - 1 + NX - 1 + 4)
    send_y(0)
    relay(0, 2)

    later[0].wait()
    acc = lax.dot_general(f_v[128:, :], d_v[...], NT, preferred_element_type=F32)
    later[1].wait()
    acc = acc + lax.dot_general(g_v[128:, :], l_v[...], NT, preferred_element_type=F32)
    pack(1, acc)
    send_y(1)

    load_c.wait()
    wide[...] = jnp.zeros_like(wide)
    c_hi = c_v[...].astype(BF16).astype(F32)
    c_lo = c_v[...] - c_hi
    for e in range(2):
        cols = slice(e * 512, (e + 1) * 512)
        for i in range(4):
            row = i * 2 + e
            wide[row : row + 1, cols] = c_hi[i : i + 1, :]
            wide[8 + row : 9 + row, cols] = c_hi[i : i + 1, :]
            wide[16 + row : 17 + row, cols] = c_lo[i : i + 1, :]
    left[...] = wide[...].T.astype(BF16)

    settle(idx_recv.at[pl.ds(0, NR - 1)], idx_sem.at[1])
    row = lax.broadcasted_iota(jnp.int32, (32, 128), 0)
    col = lax.broadcasted_iota(jnp.int32, (32, 128), 1)
    same = ((row >> 3) == (col & 3)) & ((row & 1) == ((col >> 2) & 1))
    lane = lax.broadcasted_iota(jnp.int32, (1, 128), 1) >> 3
    which = jnp.zeros((1, 128), jnp.int32)
    for s in range(NR):
        which = which + idx_recv[s] * (lane == s).astype(jnp.int32)
    match = same.astype(F32) * (which == ((row >> 1) & 3)).astype(F32)
    sel[...] = match.astype(BF16)
    for one in load_v:
        one.wait()

    def turn(t):
        settle(y_recv.at[t, pl.ds(0, NR - 1)], y_sem.at[1, t])
        arrived = y_recv[t].reshape(128, 256)
        summed = jnp.dot(sel[...], arrived, preferred_element_type=F32).astype(BF16)
        for hi in range(2):
            for to_x in X_ORDER:
                turned = lax.dot_general(summed, v_v[hi, to_x], NT, preferred_element_type=F32)
                x_send[t, hi, to_x] = turned.astype(BF16)
            for to_x in X_ORDER:
                @pl.when(x != to_x)
                def _():
                    pltpu.make_async_remote_copy(
                        src_ref=x_send.at[t, hi, to_x], dst_ref=x_recv.at[t, hi, x],
                        send_sem=x_sem.at[0, t, hi], recv_sem=x_sem.at[1, t, hi],
                        device_id=(pair, to_x * 2 + h), device_id_type=MESH,
                    ).start()
            x_recv[t, hi, x] = x_send[t, hi, x]

    def pass_on(t, hi):
        settle(x_recv.at[t, hi, pl.ds(0, NX - 1)], x_sem.at[1, t, hi])
        total = x_recv[t, hi, 0].astype(F32)
        for from_x in range(1, NX):
            total = total + x_recv[t, hi, from_x].astype(F32)
        z_send[hi, t * 4 : t * 4 + 4] = total.reshape(4, 8, 128).astype(BF16)

    def send_z(t, hi):
        for to_l in range(t * 4, t * 4 + 4):
            @pl.when(z != hi * ZL + to_l)
            def _():
                pltpu.make_async_remote_copy(
                    src_ref=z_send.at[hi, to_l], dst_ref=z_recv.at[z],
                    send_sem=z_sem.at[0], recv_sem=z_sem.at[1],
                    device_id=(to_l * NR + r, x * 2 + hi), device_id_type=MESH,
                ).start()

    pl.semaphore_wait(ready_sem.at[0], 2)
    relay(1, 4)
    turn(0)
    turn(1)
    pass_on(0, 0)
    pl.semaphore_wait(ready_sem.at[1], 2)
    send_z(0, 0)
    for t, hi in ((1, 0), (0, 1), (1, 1)):
        pass_on(t, hi)
        send_z(t, hi)
    z_recv[z] = z_send[h, l]

    settle(idx_recv.at[pl.ds(0, NR - 1)], idx_sem.at[0])
    for t in range(2):
        settle(y_recv.at[t, pl.ds(0, NR - 1)], y_sem.at[0, t])
        for hi in range(2):
            settle(x_recv.at[t, hi, pl.ds(0, NX - 1)], x_sem.at[0, t, hi])

    settle(z_recv.at[pl.ds(0, NZ - 1)], z_sem.at[1])
    got = z_recv[0].astype(F32)
    for from_z in range(1, NZ):
        got = got + z_recv[from_z].astype(F32)
    hi = got.astype(BF16).astype(F32)
    right = jnp.concatenate([hi, got - hi, hi, jnp.zeros((104, 128), F32)], axis=0).astype(BF16)
    result = jnp.dot(left[...], right, preferred_element_type=F32)
    out_ref[...] = result.astype(BF16).reshape(2, 512, 128)
    settle(z_recv.at[pl.ds(0, NZ - 1)], z_sem.at[0])


def shards(
    occupied_index,
    doubles_slab,
    lambda_slab,
    aux_factors,
    dressed_factors,
    virtual_coefs,
    occupied_coefs,
):
    dma = pltpu.SemaphoreType.DMA
    return pl.pallas_call(
        kernel,
        out_shape=pltpu.VMEM((2, 512, 128), BF16),
        in_specs=[pl.BlockSpec(memory_space=pltpu.HBM)] * 7,
        out_specs=pl.BlockSpec(memory_space=pltpu.VMEM),
        scratch_shapes=[
            pltpu.SMEM((1, 1), jnp.int32),
            pltpu.VMEM((256, 2048), BF16),
            pltpu.VMEM((256, 2048), BF16),
            pltpu.VMEM((256, 2048), BF16),
            pltpu.VMEM((256, 2048), BF16),
            pltpu.VMEM((2, NX, 128, 256), BF16),
            pltpu.VMEM((4, 512), F32),
            pltpu.VMEM((128, 128), BF16),
            pltpu.VMEM((1, 128), jnp.int32),
            pltpu.VMEM((NR, 1, 128), jnp.int32),
            pltpu.VMEM((2, NR, 8, 256), BF16),
            pltpu.VMEM((2, NR, 8, 256), BF16),
            pltpu.VMEM((32, 128), BF16),
            pltpu.VMEM((2, 2, NX, 32, 128), BF16),
            pltpu.VMEM((2, 2, NX, 32, 128), BF16),
            pltpu.VMEM((2, ZL, 8, 128), BF16),
            pltpu.VMEM((NZ, 8, 128), BF16),
            pltpu.VMEM((128, 1024), F32),
            pltpu.VMEM((1024, 128), BF16),
            dma((14,)),
            dma((2,)),
            dma((2, 2)),
            dma((2, 2, 2)),
            dma((2,)),
            pltpu.SemaphoreType.REGULAR((2,)),
        ],
        compiler_params=pltpu.CompilerParams(
            collective_id=0, has_side_effects=True, vmem_limit_bytes=60 << 20
        ),
    )(
        occupied_index.reshape(1, 1), doubles_slab, lambda_slab, aux_factors, dressed_factors,
        virtual_coefs.reshape(NX, 2, 128, 256), occupied_coefs.T,
    )


def solution(mesh):
    placed = (
        P("pair"),
        P("pair", "aux", None),
        P("pair", "aux", None),
        P("pair", None, None),
        P("pair", None, None),
        P(None, "aux"),
        P(),
    )
    return jax.shard_map(
        shards, mesh=mesh, in_specs=placed, out_specs=P("pair", None, "aux"), check_vma=False
    )
```

```python
import jax
import jax.numpy as jnp
from jax import lax
from jax.experimental import pallas as pl
from jax.experimental.pallas import tpu as pltpu
from jax.sharding import PartitionSpec as P

MESH = pl.DeviceIdType.MESH
F32, BF16 = jnp.float32, jnp.bfloat16
NT = (((1,), (1,)), ((), ()))
NX, NY, NZ, ZL = 4, 8, 16, 8
NR = 2 * NY
Y_ORDER = (0, 1, 2, 3, 7, 6, 5, 4)
X_ORDER = (0, 1, 2, 3)


def kernel(
    idx_hbm, d_hbm, l_hbm, f_hbm, g_hbm, v_hbm, c_hbm, out_ref,
    idx_s, d_v, l_v, f_v, g_v, v_v, c_v,
    order, idx_send, idx_recv, y_send, y_recv, sel, x_send, x_recv,
    z_send, z_recv, wide, left,
    load_sem, idx_sem, y_sem, x_sem, z_sem, ready_sem,
):
    pair, aux = lax.axis_index("pair"), lax.axis_index("aux")
    barrier = pltpu.get_barrier_semaphore()

    def load(src, dst, n):
        return pltpu.make_async_copy(src, dst, load_sem.at[n])

    depth = d_v.shape[1] // 2
    loads = []
    for a_hbm, a_v, b_hbm, b_v in ((f_hbm, f_v, d_hbm, d_v), (g_hbm, g_v, l_hbm, l_v)):
        for k in range(2):
            cols = pl.ds(k * depth, depth)
            top = pl.ds(0, 128)
            n = 1 + 2 * len(loads)
            loads.append((
                load(b_hbm.at[0, :, cols], b_v.at[:, cols], n),
                load(a_hbm.at[0, top, cols], a_v.at[top, cols], n + 1),
            ))
    rest = pl.ds(128, 128)
    later = [
        load(f_hbm.at[0, rest, :], f_v.at[rest, :], 9),
        load(g_hbm.at[0, rest, :], g_v.at[rest, :], 10),
    ]
    load_i = load(idx_hbm, idx_s, 0)
    load_v = [load(v_hbm.at[:, hi], v_v.at[hi], 11 + hi) for hi in range(2)]
    load_c = load(c_hbm, c_v, 13)
    for pair_of in loads:
        for one in pair_of:
            one.start()
    load_i.start()

    r = lax.rem(pair, NR)
    l = lax.div(pair, NR)
    x = lax.div(aux, 2)
    h = lax.rem(aux, 2)
    z = h * ZL + l
    row0 = l * NR

    def z_away(dz):
        to_z = lax.rem(z + (dz + NZ), NZ)
        to_h = lax.div(to_z, ZL)
        return ((to_z - to_h * ZL) * NR + r, x * 2 + to_h)

    def greet(to):
        pl.semaphore_signal(barrier, inc=1, device_id=to, device_id_type=MESH)

    for to_r in range(NR):
        @pl.when(r != to_r)
        def _():
            greet((row0 + to_r, aux))

    for to_x in range(NX):
        @pl.when(x != to_x)
        def _():
            greet((pair, to_x * 2 + h))

    greet(z_away(1))
    greet(z_away(-1))

    row = lax.broadcasted_iota(jnp.int32, (128, 128), 0)
    col = lax.broadcasted_iota(jnp.int32, (128, 128), 1)
    source = (row & 3) * 32 + (row >> 3) * 2 + ((row >> 2) & 1)
    order[...] = (source == col).astype(F32).astype(BF16)

    def pack(t, acc):
        sorted_rows = jnp.dot(order[...], acc.astype(BF16), preferred_element_type=F32)
        y_send[t] = sorted_rows.astype(BF16).reshape(NR, 8, 256)
        y_recv[t, r] = y_send[t, r]

    def send_y(t):
        for to_r in (2 * to_y + c for to_y in Y_ORDER for c in range(2)):
            @pl.when(r != to_r)
            def _():
                to = (row0 + to_r, aux)
                if t == 0:
                    pltpu.make_async_remote_copy(
                        src_ref=idx_send, dst_ref=idx_recv.at[r],
                        send_sem=idx_sem.at[0], recv_sem=idx_sem.at[1],
                        device_id=to, device_id_type=MESH,
                    ).start()
                pltpu.make_async_remote_copy(
                    src_ref=y_send.at[t, to_r], dst_ref=y_recv.at[t, r],
                    send_sem=y_sem.at[0, t], recv_sem=y_sem.at[1, t],
                    device_id=to, device_id_type=MESH,
                ).start()

    def relay(n, dz):
        for to in (z_away(dz), z_away(-dz)):
            pl.semaphore_signal(ready_sem.at[n], inc=1, device_id=to, device_id_type=MESH)

    def settle(ref, sem):
        pltpu.make_async_copy(ref, ref, sem).wait()

    acc = None
    for n, (load_b, load_a) in enumerate(loads):
        load_b.wait()
        load_a.wait()
        if n == 2:
            for one in later:
                one.start()
        if n == 3:
            for one in load_v + [load_c]:
                one.start()
        a_v, b_v = ((f_v, d_v), (g_v, l_v))[n // 2]
        cols = slice(n % 2 * depth, (n % 2 + 1) * depth)
        part = lax.dot_general(a_v[:128, cols], b_v[:, cols], NT, preferred_element_type=F32)
        acc = part if acc is None else acc + part
    pack(0, acc)
    load_i.wait()
    idx_send[...] = jnp.full((1, 128), idx_s[0, 0], jnp.int32)
    idx_recv[r] = jnp.full((1, 128), idx_s[0, 0], jnp.int32)

    pl.semaphore_wait(barrier, NR - 1 + NX - 1 + 2)
    send_y(0)
    relay(0, 1)

    later[0].wait()
    acc = lax.dot_general(f_v[128:, :], d_v[...], NT, preferred_element_type=F32)
    later[1].wait()
    acc = acc + lax.dot_general(g_v[128:, :], l_v[...], NT, preferred_element_type=F32)
    pack(1, acc)
    send_y(1)
    pl.semaphore_wait(ready_sem.at[0], 2)
    relay(1, 2)

    load_c.wait()
    wide[...] = jnp.zeros_like(wide)
    c_hi = c_v[...].astype(BF16).astype(F32)
    c_lo = c_v[...] - c_hi
    for e in range(2):
        cols = slice(e * 512, (e + 1) * 512)
        for i in range(4):
            row = i * 2 + e
            wide[row : row + 1, cols] = c_hi[i : i + 1, :]
            wide[8 + row : 9 + row, cols] = c_hi[i : i + 1, :]
            wide[16 + row : 17 + row, cols] = c_lo[i : i + 1, :]
    left[...] = wide[...].T.astype(BF16)

    settle(idx_recv.at[pl.ds(0, NR - 1)], idx_sem.at[1])
    row = lax.broadcasted_iota(jnp.int32, (32, 128), 0)
    col = lax.broadcasted_iota(jnp.int32, (32, 128), 1)
    same = ((row >> 3) == (col & 3)) & ((row & 1) == ((col >> 2) & 1))
    lane = lax.broadcasted_iota(jnp.int32, (1, 128), 1) >> 3
    which = jnp.zeros((1, 128), jnp.int32)
    for s in range(NR):
        which = which + idx_recv[s] * (lane == s).astype(jnp.int32)
    match = same.astype(F32) * (which == ((row >> 1) & 3)).astype(F32)
    sel[...] = match.astype(BF16)
    for one in load_v:
        one.wait()

    def turn(t):
        settle(y_recv.at[t, pl.ds(0, NR - 1)], y_sem.at[1, t])
        arrived = y_recv[t].reshape(128, 256)
        summed = jnp.dot(sel[...], arrived, preferred_element_type=F32).astype(BF16)
        for hi in range(2):
            for to_x in X_ORDER:
                turned = lax.dot_general(summed, v_v[hi, to_x], NT, preferred_element_type=F32)
                x_send[t, hi, to_x] = turned.astype(BF16)
            for to_x in X_ORDER:
                @pl.when(x != to_x)
                def _():
                    pltpu.make_async_remote_copy(
                        src_ref=x_send.at[t, hi, to_x], dst_ref=x_recv.at[t, hi, x],
                        send_sem=x_sem.at[0, t, hi], recv_sem=x_sem.at[1, t, hi],
                        device_id=(pair, to_x * 2 + h), device_id_type=MESH,
                    ).start()
            x_recv[t, hi, x] = x_send[t, hi, x]

    def pass_on(t, hi):
        settle(x_recv.at[t, hi, pl.ds(0, NX - 1)], x_sem.at[1, t, hi])
        total = x_recv[t, hi, 0].astype(F32)
        for from_x in range(1, NX):
            total = total + x_recv[t, hi, from_x].astype(F32)
        z_send[hi, t * 4 : t * 4 + 4] = total.reshape(4, 8, 128).astype(BF16)

    def send_z(t, hi):
        for to_l in range(t * 4, t * 4 + 4):
            @pl.when(z != hi * ZL + to_l)
            def _():
                pltpu.make_async_remote_copy(
                    src_ref=z_send.at[hi, to_l], dst_ref=z_recv.at[z],
                    send_sem=z_sem.at[0], recv_sem=z_sem.at[1],
                    device_id=(to_l * NR + r, x * 2 + hi), device_id_type=MESH,
                ).start()

    pl.semaphore_wait(ready_sem.at[1], 2)
    relay(2, 4)
    turn(0)
    turn(1)
    pass_on(0, 0)
    pl.semaphore_wait(ready_sem.at[2], 2)
    send_z(0, 0)
    for t, hi in ((1, 0), (0, 1), (1, 1)):
        pass_on(t, hi)
        send_z(t, hi)
    z_recv[z] = z_send[h, l]

    settle(idx_recv.at[pl.ds(0, NR - 1)], idx_sem.at[0])
    for t in range(2):
        settle(y_recv.at[t, pl.ds(0, NR - 1)], y_sem.at[0, t])
        for hi in range(2):
            settle(x_recv.at[t, hi, pl.ds(0, NX - 1)], x_sem.at[0, t, hi])

    settle(z_recv.at[pl.ds(0, NZ - 1)], z_sem.at[1])
    got = z_recv[0].astype(F32)
    for from_z in range(1, NZ):
        got = got + z_recv[from_z].astype(F32)
    hi = got.astype(BF16).astype(F32)
    right = jnp.concatenate([hi, got - hi, hi, jnp.zeros((104, 128), F32)], axis=0).astype(BF16)
    result = jnp.dot(left[...], right, preferred_element_type=F32)
    out_ref[...] = result.astype(BF16).reshape(2, 512, 128)
    settle(z_recv.at[pl.ds(0, NZ - 1)], z_sem.at[0])


def shards(
    occupied_index,
    doubles_slab,
    lambda_slab,
    aux_factors,
    dressed_factors,
    virtual_coefs,
    occupied_coefs,
):
    dma = pltpu.SemaphoreType.DMA
    return pl.pallas_call(
        kernel,
        out_shape=pltpu.VMEM((2, 512, 128), BF16),
        in_specs=[pl.BlockSpec(memory_space=pltpu.HBM)] * 7,
        out_specs=pl.BlockSpec(memory_space=pltpu.VMEM),
        scratch_shapes=[
            pltpu.SMEM((1, 1), jnp.int32),
            pltpu.VMEM((256, 2048), BF16),
            pltpu.VMEM((256, 2048), BF16),
            pltpu.VMEM((256, 2048), BF16),
            pltpu.VMEM((256, 2048), BF16),
            pltpu.VMEM((2, NX, 128, 256), BF16),
            pltpu.VMEM((4, 512), F32),
            pltpu.VMEM((128, 128), BF16),
            pltpu.VMEM((1, 128), jnp.int32),
            pltpu.VMEM((NR, 1, 128), jnp.int32),
            pltpu.VMEM((2, NR, 8, 256), BF16),
            pltpu.VMEM((2, NR, 8, 256), BF16),
            pltpu.VMEM((32, 128), BF16),
            pltpu.VMEM((2, 2, NX, 32, 128), BF16),
            pltpu.VMEM((2, 2, NX, 32, 128), BF16),
            pltpu.VMEM((2, ZL, 8, 128), BF16),
            pltpu.VMEM((NZ, 8, 128), BF16),
            pltpu.VMEM((128, 1024), F32),
            pltpu.VMEM((1024, 128), BF16),
            dma((14,)),
            dma((2,)),
            dma((2, 2)),
            dma((2, 2, 2)),
            dma((2,)),
            pltpu.SemaphoreType.REGULAR((3,)),
        ],
        compiler_params=pltpu.CompilerParams(
            collective_id=0, has_side_effects=True, vmem_limit_bytes=60 << 20
        ),
    )(
        occupied_index.reshape(1, 1), doubles_slab, lambda_slab, aux_factors, dressed_factors,
        virtual_coefs.reshape(NX, 2, 128, 256), occupied_coefs.T,
    )


def solution(mesh):
    placed = (
        P("pair"),
        P("pair", "aux", None),
        P("pair", "aux", None),
        P("pair", None, None),
        P("pair", None, None),
        P(None, "aux"),
        P(),
    )
    return jax.shard_map(
        shards, mesh=mesh, in_specs=placed, out_specs=P("pair", None, "aux"), check_vma=False
    )
```
